32 devices in a mesh: frames: 8 (over y, x, core), rows: 4 (over z).
Axes of the slice: x: 2, y: 2, z: 4, core: 2. Of those that a mesh axis runs over, the one named last changes fastest.
Arguments:
- video: bfloat16 [8, 16, 320, 192], P('frames', 'rows'), may hold values from -6 to 6
- spatial_weights: bfloat16 [4, 3, 3, 192, 192], replicated, may hold values from -0.15625 to 0.15625
- norm_gains: float32 [4, 192], replicated, may hold values from 0.5 to 1.5
- temporal_weights: bfloat16 [2, 3, 192, 192], replicated, may hold values from -0.25 to 0.25
Outputs:
- decoded: bfloat16 [8, 16, 320, 192], P('frames', 'rows')
The draws below stay inside these ranges and needn't reach their ends.
All inputs are finite; a program needn't handle non-finite values.
Results may differ from the reference program's by a relative error of at most 0.013.
Values may be sent and summed in bfloat16 or wider, within the bound.
A program may use at most 64 MiB of HBM per device.

```python
import jax
import jax.numpy as jnp
from jax import lax

C = 192
W = 320
BLOCKS = 2
H = 16
FRAMES = 8


def level_of(stream_key, extent, pieces, low, high):
    def one(axis_at, shards_of):
        draws = jax.random.uniform(jax.random.fold_in(jax.random.fold_in(stream_key, 6), axis_at), (shards_of,), jnp.float32, low / len(pieces), high / len(pieces))
        return jnp.repeat(jnp.exp(draws), extent[axis_at] // shards_of).reshape((-1,) + (1,) * (len(extent) - axis_at - 1))

    factor_of = one(*pieces[0])
    for cut in pieces[1:]:
        factor_of = factor_of * one(*cut)
    return factor_of


def scatter_about(stream_key, shape, deviation, limit, cuts=(), kind=jnp.bfloat16):
    array = jax.random.normal(stream_key, shape, jnp.float32) * deviation
    if len(cuts) > 0:
        array = level_of(stream_key, shape, cuts, -0.22, 0.18) * array
    return jnp.clip(array, min=-limit, max=limit).astype(kind)


def setup_inputs(seed: int = 0) -> dict:
    keys = jax.random.split(jax.random.key(seed), 5)
    video = scatter_about(keys[0], (FRAMES, H, W, C), 1.0, 6.0, ((0, 8), (1, 4)))
    spatial_weights = scatter_about(keys[1], (2 * BLOCKS, 3, 3, C, C), (9 * C) ** -0.5, 0.15625)
    norm_gains = jnp.clip(jax.random.uniform(keys[2], (2 * BLOCKS, C), jnp.float32, 0.5, 1.5), 0.5, 1.5)
    temporal_weights = scatter_about(keys[3], (BLOCKS, 3, C, C), (3 * C) ** -0.5, 0.25)
    return {"video": video, "spatial_weights": spatial_weights, "norm_gains": norm_gains, "temporal_weights": temporal_weights}


epsilon = 1e-06

def normed(values, gain):
    values = values.astype(jnp.float32)
    mean_sq = lax.optimization_barrier(jnp.mean(values * values, axis=-1, keepdims=True))
    scaled = values * lax.rsqrt(mean_sq + epsilon) * gain.astype(jnp.float32)
    return jax.nn.silu(scaled).astype(jnp.bfloat16)

def conv_frame(active, kernel):
    height, width, channels = active.shape
    padded = jnp.pad(active.astype(jnp.float32), ((1, 1), (1, 1), (0, 0)))
    total = jnp.zeros((height * width, kernel.shape[-1]), jnp.float32)
    for row_step in range(3):
        for col_step in range(3):
            window = padded[row_step:row_step + height, col_step:col_step + width].reshape(-1, channels)
            total = total + jnp.dot(window, kernel[row_step, col_step].astype(jnp.float32), preferred_element_type=jnp.float32)
    return total.reshape(height, width, kernel.shape[-1])

def reference(video, spatial_weights, norm_gains, temporal_weights):
    current = video
    for block in range(BLOCKS):

        def spatial(frame):
            first = conv_frame(normed(frame, norm_gains[2 * block]), spatial_weights[2 * block]).astype(jnp.bfloat16)
            second = conv_frame(normed(first, norm_gains[2 * block + 1]), spatial_weights[2 * block + 1])
            return (frame.astype(jnp.float32) + second).astype(jnp.bfloat16)
        inner = lax.map(spatial, current)
        padded = jnp.concatenate([jnp.zeros((2,) + inner.shape[1:], jnp.bfloat16), inner], axis=0)

        def temporal(index):
            taps = lax.dynamic_slice_in_dim(padded, index, 3, 0)
            height, width, channels = taps.shape[1:]
            total = taps[2].astype(jnp.float32).reshape(-1, channels)
            for offset in range(3):
                total = total + jnp.dot(taps[2 - offset].astype(jnp.float32).reshape(-1, channels), temporal_weights[block, offset].astype(jnp.float32), preferred_element_type=jnp.float32)
            return total.reshape(height, width, channels).astype(jnp.bfloat16)
        current = lax.map(temporal, jnp.arange(inner.shape[0], dtype=jnp.int32))
    return current
```

```python
import functools

import jax
import jax.numpy as jnp
from jax import lax
from jax.experimental import pallas as pl
from jax.experimental.pallas import tpu as pltpu
from jax.sharding import PartitionSpec as P

epsilon = 1e-06
MESH = pl.DeviceIdType.MESH


def kernel(
    frames,
    strips,
    video_ref,
    weights_ref,
    gains_ref,
    taps_ref,
    out_ref,
    cur,
    act,
    act2,
    inner,
    one_back,
    two_back,
    weights,
    local_sem,
    halo_send,
    halo_recv,
    two_send,
    two_recv,
    one_send,
    one_recv,
):
    f = lax.axis_index("frames")
    z = lax.axis_index("rows")
    blocks, rows, width, channels = inner.shape
    pad = act.shape[-1] // 3
    odd = lax.rem(f, 2)
    even_dev = odd == 0
    pair = f + 1 - 2 * odd
    has_up, has_down = z > 0, z < strips - 1
    has_next, has_prev = f < frames - 2, f > 1
    has_one = f > 0
    gives_one = jnp.logical_or(even_dev, has_prev)

    own = pltpu.make_async_copy(
        video_ref.at[0], cur.at[0, pl.ds(2, rows)], local_sem.at[0]
    )
    own.start()
    loads = []
    for k in range(2 * blocks):
        load = pltpu.make_async_copy(
            weights_ref.at[k],
            weights.at[k, :, :, pl.ds(0, channels), :],
            local_sem.at[1 + k],
        )
        load.start()
        loads.append(load)

    barrier = pltpu.get_barrier_semaphore()
    count = jnp.int32(1)
    pl.semaphore_signal(barrier, inc=1, device_id={"frames": pair}, device_id_type=MESH)
    for present, where in (
        (has_up, {"rows": z - 1}),
        (has_down, {"rows": z + 1}),
        (has_next, {"frames": f + 2}),
        (has_prev, {"frames": f - 2}),
    ):
        count = count + jnp.where(present, 1, 0)

        @pl.when(present)
        def _():
            pl.semaphore_signal(barrier, inc=1, device_id=where, device_id_type=MESH)

    pl.semaphore_wait(barrier, count)

    def up_copy(b, i):
        source = video_ref.at[0, i] if b == 0 else cur.at[b, 2 + i]
        return pltpu.make_async_remote_copy(
            src_ref=source,
            dst_ref=cur.at[b, rows + 2 + i],
            send_sem=halo_send.at[b, 0, i],
            recv_sem=halo_recv.at[b, 0, i],
            device_id={"rows": z - 1},
            device_id_type=MESH,
        )

    def down_copy(b, i):
        source = video_ref.at[0, rows - 2 + i] if b == 0 else cur.at[b, rows + i]
        return pltpu.make_async_remote_copy(
            src_ref=source,
            dst_ref=cur.at[b, i],
            send_sem=halo_send.at[b, 1, i],
            recv_sem=halo_recv.at[b, 1, i],
            device_id={"rows": z + 1},
            device_id_type=MESH,
        )

    def two_copy(b, r):
        return pltpu.make_async_remote_copy(
            src_ref=inner.at[b, r],
            dst_ref=two_back.at[b, r],
            send_sem=two_send.at[b, r],
            recv_sem=two_recv.at[b, r],
            device_id={"frames": f + 2},
            device_id_type=MESH,
        )

    def one_copy(source, b, r):
        return pltpu.make_async_remote_copy(
            src_ref=source.at[b, r],
            dst_ref=one_back.at[b, r],
            send_sem=one_send.at[b, r],
            recv_sem=one_recv.at[b, r],
            device_id={"frames": pair},
            device_id_type=MESH,
        )

    def when(present, action):
        pl.when(present)(action)

    for i in (1, 0):
        when(has_up, lambda: up_copy(0, 1 - i).start())
        when(has_down, lambda: down_copy(0, i).start())

    def clear(ref, b):
        def row(r, carry):
            ref[b, r] = jnp.zeros((width, channels), jnp.bfloat16)
            return carry

        lax.fori_loop(0, rows, row, 0)

    for b in range(blocks):

        @pl.when(jnp.logical_not(has_up))
        def _():
            for i in range(2):
                cur[b, i] = jnp.zeros((width, channels), jnp.bfloat16)

        @pl.when(jnp.logical_not(has_down))
        def _():
            for i in range(2):
                cur[b, rows + 2 + i] = jnp.zeros((width, channels), jnp.bfloat16)

        @pl.when(jnp.logical_not(has_prev))
        def _():
            clear(two_back, b)

        @pl.when(jnp.logical_not(has_one))
        def _():
            clear(one_back, b)

    if pad > channels:

        def clear_pad(buffer, count):
            def row(r, carry):
                for step in range(3):
                    buffer[r, :, step * pad + channels : (step + 1) * pad] = jnp.zeros(
                        (width, pad - channels), jnp.bfloat16
                    )
                return carry

            lax.fori_loop(0, count, row, 0)

        clear_pad(act, rows + 4)
        clear_pad(act2, rows + 2)

        def clear_weights(k, carry):
            for di in range(3):
                for dj in range(3):
                    weights[k, di, dj, channels:pad, :] = jnp.zeros(
                        (pad - channels, channels), jnp.bfloat16
                    )
            return carry

        lax.fori_loop(0, 2 * blocks, clear_weights, 0)

    column = lax.broadcasted_iota(jnp.int32, (width, channels), 0)

    def store_active(buffer, index, values, gain):
        mean_sq = jnp.mean(values * values, axis=-1, keepdims=True)
        half = values * lax.rsqrt(mean_sq + epsilon) * (0.5 * gain)
        active = half + half * jnp.tanh(half)
        before = jnp.where(column == 0, 0.0, pltpu.roll(active, 1, 0))
        after = jnp.where(column == width - 1, 0.0, pltpu.roll(active, width - 1, 0))
        buffer[index, :, 0:channels] = before.astype(jnp.bfloat16)
        buffer[index, :, pad : pad + channels] = active.astype(jnp.bfloat16)
        buffer[index, :, 2 * pad : 2 * pad + channels] = after.astype(jnp.bfloat16)

    def conv_row(buffer, index, k):
        total = None
        for di in range(3):
            term = jnp.dot(
                buffer[index + di],
                weights[k, di].reshape(3 * pad, channels),
                preferred_element_type=jnp.float32,
            )
            total = term if total is None else total + term
        return total

    def loop(count, body):
        def step(i, carry):
            body(i)
            return carry

        lax.fori_loop(0, count, step, 0)

    own.wait()
    for b in range(blocks):
        gain_a = gains_ref[2 * b : 2 * b + 1, :]
        gain_b = gains_ref[2 * b + 1 : 2 * b + 2, :]

        def active_row(index):
            store_active(act, index, cur[b, index].astype(jnp.float32), gain_a)

        def first_row(index, valid=None):
            first = conv_row(act, index, 2 * b)
            if valid is not None:
                first = jnp.where(valid, first, 0.0)
            first = first.astype(jnp.bfloat16).astype(jnp.float32)
            store_active(act2, index, first, gain_b)

        def inner_row(r):
            second = conv_row(act2, r, 2 * b + 1)
            inner[b, r] = (cur[b, 2 + r].astype(jnp.float32) + second).astype(jnp.bfloat16)
            when(has_next, lambda: two_copy(b, r).start())
            when(even_dev, lambda: one_copy(inner, b, r).start())

        loop(rows, lambda i: active_row(2 + i))
        loads[2 * b].wait()
        loop(rows - 2, lambda i: first_row(2 + i))
        when(has_down, lambda: up_copy(b, 0).wait_recv())
        when(has_up, lambda: down_copy(b, 1).wait_recv())
        loop(2, lambda i: active_row(1 + i * (rows + 1)))
        loop(2, lambda i: first_row(1 + i * (rows - 1)))
        loads[2 * b + 1].wait()
        loop(rows - 2, lambda i: inner_row(1 + i))
        when(has_down, lambda: up_copy(b, 1).wait_recv())
        when(has_up, lambda: down_copy(b, 0).wait_recv())
        loop(2, lambda i: active_row(i * (rows + 3)))
        loop(
            2,
            lambda i: first_row(
                i * (rows + 1),
                jnp.where(i == 0, z, strips - 1 - z) > 0,
            ),
        )
        loop(2, lambda i: inner_row(i * (rows - 1)))

        def decode_row(r):
            @pl.when(has_prev)
            def _():
                two_copy(b, r).wait_recv()

                @pl.when(odd == 1)
                def _():
                    one_copy(two_back, b, r).start()

            when(has_one, lambda: one_copy(inner, b, r).wait_recv())
            mine = inner[b, r]
            total = mine.astype(jnp.float32)
            for k, taken in enumerate((mine, one_back[b, r], two_back[b, r])):
                total = total + jnp.dot(
                    taken, taps_ref[b, k], preferred_element_type=jnp.float32
                )
            total = total.astype(jnp.bfloat16)
            if b == blocks - 1:
                out_ref[0, r] = total
            else:
                cur[b + 1, 2 + r] = total

        def share(r):
            if b < blocks - 1:
                if r < 2:
                    when(has_up, lambda: up_copy(b + 1, r).start())
                if r >= rows - 2:
                    when(has_down, lambda: down_copy(b + 1, r - rows + 2).start())

        if b == blocks - 1:
            loop(rows - 2, lambda i: decode_row(1 + i))
            loop(2, lambda i: decode_row(i * (rows - 1)))
        else:
            for r in list(range(1, rows - 1)) + [0, rows - 1]:
                decode_row(r)
                share(r)

    for b in range(blocks):
        for i in range(2):
            when(has_up, lambda: up_copy(b, i).wait_send())
            when(has_down, lambda: down_copy(b, i).wait_send())
        for r in range(rows):
            when(has_next, lambda: two_copy(b, r).wait_send())
            when(gives_one, lambda: one_copy(inner, b, r).wait_send())


def solution(mesh):
    frames, strips = mesh.shape["frames"], mesh.shape["rows"]

    def on_device(video, spatial_weights, norm_gains, temporal_weights):
        held, rows, width, channels = video.shape
        blocks = temporal_weights.shape[0]
        assert held == 1 and rows > 2 and frames % 2 == 0
        pad = -(-channels // 256) * 256
        strip = (blocks, rows, width, channels)
        any_space = pl.BlockSpec(memory_space=pl.ANY)
        vmem = pl.BlockSpec(memory_space=pltpu.VMEM)
        dma = pltpu.SemaphoreType.DMA
        return pl.pallas_call(
            functools.partial(kernel, frames, strips),
            out_shape=jax.ShapeDtypeStruct(video.shape, video.dtype),
            in_specs=[any_space, any_space, vmem, vmem],
            out_specs=vmem,
            scratch_shapes=[
                pltpu.VMEM((blocks, rows + 4, width, channels), jnp.bfloat16),
                pltpu.VMEM((rows + 4, width, 3 * pad), jnp.bfloat16),
                pltpu.VMEM((rows + 2, width, 3 * pad), jnp.bfloat16),
                pltpu.VMEM(strip, jnp.bfloat16),
                pltpu.VMEM(strip, jnp.bfloat16),
                pltpu.VMEM(strip, jnp.bfloat16),
                pltpu.VMEM((2 * blocks, 3, 3, pad, channels), jnp.bfloat16),
                dma((1 + 2 * blocks,)),
                dma((blocks, 2, 2)),
                dma((blocks, 2, 2)),
                dma((blocks, rows)),
                dma((blocks, rows)),
                dma((blocks, rows)),
                dma((blocks, rows)),
            ],
            compiler_params=pltpu.CompilerParams(
                collective_id=0, has_side_effects=True, vmem_limit_bytes=48 << 20
            ),
        )(video, spatial_weights, norm_gains, temporal_weights)

    placed = (P("frames", "rows", None, None), P(), P(), P())
    return jax.shard_map(
        on_device,
        mesh=mesh,
        in_specs=placed,
        out_specs=P("frames", "rows", None, None),
        check_vma=False,
    )
```

```python
import functools

import jax
import jax.numpy as jnp
from jax import lax
from jax.experimental import pallas as pl
from jax.experimental.pallas import tpu as pltpu
from jax.sharding import PartitionSpec as P

epsilon = 1e-06
MESH = pl.DeviceIdType.MESH


def kernel(
    frames,
    strips,
    video_ref,
    weights_ref,
    gains_ref,
    taps_ref,
    out_ref,
    cur,
    act,
    act2,
    inner,
    packed,
    one_back,
    two_back,
    weights,
    gains,
    taps,
    local_sem,
    small_sem,
    halo_send,
    halo_recv,
    two_send,
    two_recv,
    one_send,
    one_recv,
):
    f = lax.axis_index("frames")
    z = lax.axis_index("rows")
    blocks, rows, width, channels = inner.shape
    pad = act.shape[-1] // 3
    lanes = packed.shape[-1]
    middle = width // 2
    odd = lax.rem(f, 2)
    even_dev = odd == 0
    pair = f + 1 - 2 * odd
    has_up, has_down = z > 0, z < strips - 1
    has_next, has_prev = f < frames - 2, f > 1
    has_one = f > 0
    gives_one = jnp.logical_or(even_dev, has_prev)

    own = pltpu.make_async_copy(
        video_ref.at[0], cur.at[0, pl.ds(2, rows)], local_sem.at[0]
    )
    own.start()
    loads = []
    for k in range(2 * blocks):
        load = pltpu.make_async_copy(
            weights_ref.at[k],
            weights.at[k, :, :, pl.ds(0, channels), :],
            local_sem.at[1 + k],
        )
        load.start()
        loads.append(load)

    gains_load = pltpu.make_async_copy(gains_ref, gains, small_sem.at[0])
    gains_load.start()
    taps_load = pltpu.make_async_copy(taps_ref, taps, small_sem.at[1])
    taps_load.start()

    barrier = pltpu.get_barrier_semaphore()
    count = jnp.int32(1)
    pl.semaphore_signal(barrier, inc=1, device_id={"frames": pair}, device_id_type=MESH)
    for present, where in (
        (has_up, {"rows": z - 1}),
        (has_down, {"rows": z + 1}),
        (has_next, {"frames": f + 2}),
        (has_prev, {"frames": f - 2}),
    ):
        count = count + jnp.where(present, 1, 0)

        @pl.when(present)
        def _():
            pl.semaphore_signal(barrier, inc=1, device_id=where, device_id_type=MESH)

    pl.semaphore_wait(barrier, count)

    def up_copy(b, i):
        source = video_ref.at[0, i] if b == 0 else cur.at[b, 2 + i]
        return pltpu.make_async_remote_copy(
            src_ref=source,
            dst_ref=cur.at[b, rows + 2 + i],
            send_sem=halo_send.at[b, 0, i],
            recv_sem=halo_recv.at[b, 0, i],
            device_id={"rows": z - 1},
            device_id_type=MESH,
        )

    def down_copy(b, i):
        source = video_ref.at[0, rows - 2 + i] if b == 0 else cur.at[b, rows + i]
        return pltpu.make_async_remote_copy(
            src_ref=source,
            dst_ref=cur.at[b, i],
            send_sem=halo_send.at[b, 1, i],
            recv_sem=halo_recv.at[b, 1, i],
            device_id={"rows": z + 1},
            device_id_type=MESH,
        )

    def two_copy(b, r):
        return pltpu.make_async_remote_copy(
            src_ref=packed.at[b, r],
            dst_ref=two_back.at[b, r],
            send_sem=two_send.at[b, r],
            recv_sem=two_recv.at[b, r],
            device_id={"frames": f + 2},
            device_id_type=MESH,
        )

    def one_copy(source, b, r):
        return pltpu.make_async_remote_copy(
            src_ref=source.at[b, r],
            dst_ref=one_back.at[b, r],
            send_sem=one_send.at[b, r],
            recv_sem=one_recv.at[b, r],
            device_id={"frames": pair},
            device_id_type=MESH,
        )

    def when(present, action):
        pl.when(present)(action)

    for i in (1, 0):
        when(has_up, lambda: up_copy(0, 1 - i).start())
        when(has_down, lambda: down_copy(0, i).start())

    def clear(ref, b):
        def row(r, carry):
            ref[b, r] = jnp.zeros(ref.shape[2:], jnp.bfloat16)
            return carry

        lax.fori_loop(0, rows, row, 0)

    for b in range(blocks):

        @pl.when(jnp.logical_not(has_up))
        def _():
            for i in range(2):
                cur[b, i] = jnp.zeros((width, channels), jnp.bfloat16)

        @pl.when(jnp.logical_not(has_down))
        def _():
            for i in range(2):
                cur[b, rows + 2 + i] = jnp.zeros((width, channels), jnp.bfloat16)

        @pl.when(jnp.logical_not(has_prev))
        def _():
            clear(two_back, b)

        @pl.when(jnp.logical_not(has_one))
        def _():
            clear(one_back, b)

    if pad > channels:

        def clear_pad(buffer, count):
            def row(r, carry):
                for step in range(3):
                    buffer[r, :, step * pad + channels : (step + 1) * pad] = jnp.zeros(
                        (width, pad - channels), jnp.bfloat16
                    )
                return carry

            lax.fori_loop(0, count, row, 0)

        clear_pad(act, rows + 4)
        clear_pad(act2, rows + 2)

        def clear_weights(k, carry):
            for di in range(3):
                for dj in range(3):
                    weights[k, di, dj, channels:pad, :] = jnp.zeros(
                        (pad - channels, channels), jnp.bfloat16
                    )
            return carry

        lax.fori_loop(0, 2 * blocks, clear_weights, 0)

    column = lax.broadcasted_iota(jnp.int32, (width, channels), 0)

    def store_active(buffer, index, values, gain):
        mean_sq = jnp.mean(values * values, axis=-1, keepdims=True)
        half = values * lax.rsqrt(mean_sq + epsilon) * (0.5 * gain)
        active = half + half * jnp.tanh(half)
        before = jnp.where(column == 0, 0.0, pltpu.roll(active, 1, 0))
        after = jnp.where(column == width - 1, 0.0, pltpu.roll(active, width - 1, 0))
        buffer[index, :, 0:channels] = before.astype(jnp.bfloat16)
        buffer[index, :, pad : pad + channels] = active.astype(jnp.bfloat16)
        buffer[index, :, 2 * pad : 2 * pad + channels] = after.astype(jnp.bfloat16)

    def conv_row(buffer, index, k):
        total = None
        for di in range(3):
            term = jnp.dot(
                buffer[index + di],
                weights[k, di].reshape(3 * pad, channels),
                preferred_element_type=jnp.float32,
            )
            total = term if total is None else total + term
        return total

    def loop(count, body):
        def step(i, carry):
            body(i)
            return carry

        lax.fori_loop(0, count, step, 0)

    own.wait()
    gains_load.wait()
    for b in range(blocks):
        gain_a = gains[2 * b : 2 * b + 1, :]
        gain_b = gains[2 * b + 1 : 2 * b + 2, :]

        def active_row(index):
            store_active(act, index, cur[b, index].astype(jnp.float32), gain_a)

        def first_row(index, valid=None):
            first = conv_row(act, index, 2 * b)
            if valid is not None:
                first = jnp.where(valid, first, 0.0)
            first = first.astype(jnp.bfloat16).astype(jnp.float32)
            store_active(act2, index, first, gain_b)

        def inner_row(r):
            second = conv_row(act2, r, 2 * b + 1)
            value = cur[b, 2 + r].astype(jnp.float32) + second
            inner[b, r] = value.astype(jnp.bfloat16)
            packed[b, r, 0:width, :] = value[:, 0:lanes].astype(jnp.bfloat16)
            rest = value[:, lanes:channels]
            packed[b, r, width : width + middle, :] = jnp.concatenate(
                [rest[0:middle], rest[middle:width]], axis=1
            ).astype(jnp.bfloat16)
            when(has_next, lambda: two_copy(b, r).start())
            when(even_dev, lambda: one_copy(packed, b, r).start())

        loop(rows, lambda i: active_row(2 + i))
        loads[2 * b].wait()
        loop(rows - 2, lambda i: first_row(2 + i))
        when(has_down, lambda: up_copy(b, 0).wait_recv())
        when(has_up, lambda: down_copy(b, 1).wait_recv())
        loop(2, lambda i: active_row(1 + i * (rows + 1)))
        loop(2, lambda i: first_row(1 + i * (rows - 1)))
        loads[2 * b + 1].wait()
        loop(rows - 2, lambda i: inner_row(1 + i))
        when(has_down, lambda: up_copy(b, 1).wait_recv())
        when(has_up, lambda: down_copy(b, 0).wait_recv())
        loop(2, lambda i: active_row(i * (rows + 3)))
        loop(
            2,
            lambda i: first_row(
                i * (rows + 1),
                jnp.where(i == 0, z, strips - 1 - z) > 0,
            ),
        )
        loop(2, lambda i: inner_row(i * (rows - 1)))

        if b == 0:
            taps_load.wait()

        def decode_row(r):
            @pl.when(has_prev)
            def _():
                two_copy(b, r).wait_recv()

                @pl.when(odd == 1)
                def _():
                    one_copy(two_back, b, r).start()

            when(has_one, lambda: one_copy(packed, b, r).wait_recv())
            mine = inner[b, r]
            total = mine.astype(jnp.float32)
            total = total + jnp.dot(
                mine, taps[b, 0], preferred_element_type=jnp.float32
            )
            for k, back in ((1, one_back), (2, two_back)):
                total = total + jnp.dot(
                    back[b, r, 0:width, :],
                    taps[b, k, 0:lanes, :],
                    preferred_element_type=jnp.float32,
                )
                rest = back[b, r, width : width + middle, :]
                tap = taps[b, k, lanes:channels, :]
                blank = jnp.zeros_like(tap)
                halves = [
                    jnp.dot(
                        rest,
                        jnp.concatenate(side, axis=0),
                        preferred_element_type=jnp.float32,
                    )
                    for side in ([tap, blank], [blank, tap])
                ]
                total = total + jnp.concatenate(halves, axis=0)
            total = total.astype(jnp.bfloat16)
            if b == blocks - 1:
                out_ref[0, r] = total
            else:
                cur[b + 1, 2 + r] = total

        def share(r):
            if b < blocks - 1:
                if r < 2:
                    when(has_up, lambda: up_copy(b + 1, r).start())
                if r >= rows - 2:
                    when(has_down, lambda: down_copy(b + 1, r - rows + 2).start())

        if b == blocks - 1:
            loop(rows - 2, lambda i: decode_row(1 + i))
            loop(2, lambda i: decode_row(i * (rows - 1)))
        else:
            for r in list(range(1, rows - 1)) + [0, rows - 1]:
                decode_row(r)
                share(r)

    for b in range(blocks):
        for i in range(2):
            when(has_up, lambda: up_copy(b, i).wait_send())
            when(has_down, lambda: down_copy(b, i).wait_send())
        for r in range(rows):
            when(has_next, lambda: two_copy(b, r).wait_send())
            when(gives_one, lambda: one_copy(packed, b, r).wait_send())


def solution(mesh):
    frames, strips = mesh.shape["frames"], mesh.shape["rows"]

    def on_device(video, spatial_weights, norm_gains, temporal_weights):
        held, rows, width, channels = video.shape
        blocks = temporal_weights.shape[0]
        assert held == 1 and rows > 2 and frames % 2 == 0
        pad = -(-channels // 256) * 256
        strip = (blocks, rows, width, channels)
        lanes = channels * 2 // 3
        assert 2 * (channels - lanes) == lanes
        sent = (blocks, rows, width + width // 2, lanes)
        any_space = pl.BlockSpec(memory_space=pltpu.HBM)
        vmem = pl.BlockSpec(memory_space=pltpu.VMEM)
        dma = pltpu.SemaphoreType.DMA
        return pl.pallas_call(
            functools.partial(kernel, frames, strips),
            out_shape=jax.ShapeDtypeStruct(video.shape, video.dtype),
            in_specs=[any_space] * 4,
            out_specs=vmem,
            scratch_shapes=[
                pltpu.VMEM((blocks, rows + 4, width, channels), jnp.bfloat16),
                pltpu.VMEM((rows + 4, width, 3 * pad), jnp.bfloat16),
                pltpu.VMEM((rows + 2, width, 3 * pad), jnp.bfloat16),
                pltpu.VMEM(strip, jnp.bfloat16),
                pltpu.VMEM(sent, jnp.bfloat16),
                pltpu.VMEM(sent, jnp.bfloat16),
                pltpu.VMEM(sent, jnp.bfloat16),
                pltpu.VMEM((2 * blocks, 3, 3, pad, channels), jnp.bfloat16),
                pltpu.VMEM(norm_gains.shape, jnp.float32),
                pltpu.VMEM(temporal_weights.shape, jnp.bfloat16),
                dma((1 + 2 * blocks,)),
                dma((2,)),
                dma((blocks, 2, 2)),
                dma((blocks, 2, 2)),
                dma((blocks, rows)),
                dma((blocks, rows)),
                dma((blocks, rows)),
                dma((blocks, rows)),
            ],
            compiler_params=pltpu.CompilerParams(
                collective_id=0, has_side_effects=True, vmem_limit_bytes=67043328
            ),
        )(video, spatial_weights, norm_gains, temporal_weights)

    placed = (P("frames", "rows", None, None), P(), P(), P())
    return jax.shard_map(
        on_device,
        mesh=mesh,
        in_specs=placed,
        out_specs=P("frames", "rows", None, None),
        check_vma=False,
    )
```
